32 devices in a mesh: shard: 2 (over y), ctx: 4 (over x, core), tensor: 4 (over z).
Axes of the slice: x: 2, y: 2, z: 4, core: 2. Of those that a mesh axis runs over, the one named last changes fastest.
Arguments:
- inputs: bfloat16 [2, 1024, 2048], P('shard', 'ctx'), may hold values from -6 to 6
- cotangent: bfloat16 [2, 1024, 2048], P('shard', 'ctx'), may hold values from -6 to 6
- piece_starts: int32 [2, 3], P('shard'), may hold values from 0 to 768, as said below
- positions: int32 [2, 1024], P('shard', 'ctx'), may hold values from 0 to 303, as said below
- w_qkv: float32 [2048, 8, 768], P(('shard', 'ctx'), 'tensor'), may hold values from -0.125 to 0.125
- b_qkv: float32 [8, 768], P('tensor'), may hold values from -1.2 to 1.2
- w_dense: float32 [2048, 8, 256], P(('shard', 'ctx'), 'tensor'), may hold values from -0.5 to 0.5
- w_fc1: float32 [2048, 8192], P(('shard', 'ctx'), 'tensor'), may hold values from -0.125 to 0.125
- b_fc1: float32 [8192], P('tensor'), may hold values from -3 to 3
- w_fc2: float32 [2048, 8192], P(('shard', 'ctx'), 'tensor'), may hold values from -0.0625 to 0.0625
- out_bias: float32 [2048], replicated, may hold values from -3 to 3
- ln1_gain: float32 [2048], replicated, may hold values from 0.1 to 1.9
- ln1_bias: float32 [2048], replicated, may hold values from -2 to 2
- ln2_gain: float32 [2048], replicated, may hold values from 0.1 to 1.9
- ln2_bias: float32 [2048], replicated, may hold values from -2 to 2
Outputs:
- output: bfloat16 [2, 1024, 2048], P('shard', 'ctx')
- grad_inputs: float32 [2, 1024, 2048], P('shard', 'ctx')
- grad_w_qkv: float32 [2048, 8, 768], P(('shard', 'ctx'), 'tensor')
- grad_b_qkv: float32 [8, 768], P('tensor')
- grad_w_dense: float32 [2048, 8, 256], P(('shard', 'ctx'), 'tensor')
- grad_w_fc1: float32 [2048, 8192], P(('shard', 'ctx'), 'tensor')
- grad_b_fc1: float32 [8192], P('tensor')
- grad_w_fc2: float32 [2048, 8192], P(('shard', 'ctx'), 'tensor')
- grad_out_bias: float32 [2048], replicated
- grad_ln1_gain: float32 [2048], replicated
- grad_ln1_bias: float32 [2048], replicated
- grad_ln2_gain: float32 [2048], replicated
- grad_ln2_bias: float32 [2048], replicated
The draws below stay inside these ranges and needn't reach their ends.
Inputs may be any that keep to these rules, and one draw needn't show every extreme that they name: `piece_starts`: for each sequence, 3 starts in increasing order; its picture pieces of 256 tokens do not intersect and lie inside the sequence. `positions`: in each sequence the position starts at 0 and rises by one at every token outside the picture pieces and at the first of every 16 tokens of a piece; the other tokens of a piece keep the position before them.
All inputs are finite; a program needn't handle non-finite values.
Results may differ from the reference program's by a relative error of at most 0.012.
Values may be sent and summed in bfloat16 or wider, within the bound.
No kernel may reach another device: no remote copies, remote signals or barrier semaphores. Data moves between devices by JAX's collectives and lax.ppermute only.
A program may use at most 256 MiB of HBM per device.

```python
import jax
import jax.numpy as jnp
from jax import lax

D = 2048
HEADS = 8
HEAD = 256
FF = 8192
ROT = 64
PIECE = 256
GRID = 16
PIECES = 3
LENGTH = 1024
SEQS = 2


def piece_layout(key):
    base_key = jax.random.fold_in(key, 7)
    text_count = LENGTH - PIECES * PIECE
    cut_points = jnp.sort(jax.random.randint(base_key, (SEQS, PIECES), 0, text_count + 1), axis=1)
    row_ids = jnp.arange(SEQS)[:, None]
    col_ids = jnp.arange(PIECES)[None, :]
    cut_points = jnp.where((row_ids == 0) & (col_ids == PIECES - 1), text_count, cut_points)
    cut_points = jnp.where((row_ids == 1) & (col_ids == 0), 0, cut_points)
    starts = (cut_points + col_ids * PIECE).astype(jnp.int32)
    token_index = jnp.arange(LENGTH)[None, :, None]
    inside = (token_index >= starts[:, None, :]) & (token_index < starts[:, None, :] + PIECE)
    offset = token_index - starts[:, None, :]
    row_head = jnp.any(inside & (offset % GRID == 0), axis=2)
    covered = jnp.any(inside, axis=2)
    steps_up = jnp.where(covered, row_head, True).astype(jnp.int32)
    places = (jnp.cumsum(steps_up, axis=1) - 1).astype(jnp.int32)
    return (starts, places)


def draw_piece_starts(key, part):
    return piece_layout(key)[0]


def draw_positions(key, part):
    return piece_layout(key)[1]


def strengthened(array, own_key, source, target, blocks, factor):
    def block_of(position):
        return (jnp.arange(array.shape[position]) // (array.shape[position] // blocks)).reshape((-1,) + (1,) * (array.ndim - 1 - position))

    first = jax.random.permutation(own_key, blocks)[block_of(target)]
    far = (block_of(target) + blocks // 2) % blocks
    return jnp.where((block_of(source) == first) | (block_of(source) == far), factor * array, array)


def levels(stream_key, extent, pieces, low, top_value):
    def one(position, shards_of):
        draws = jax.random.uniform(jax.random.fold_in(jax.random.fold_in(stream_key, 6), position), (shards_of,), jnp.float32, low / len(pieces), top_value / len(pieces))
        return jnp.repeat(jnp.exp(draws), extent[position] // shards_of).reshape((-1,) + (1,) * (len(extent) - position - 1))

    gain = one(*pieces[0])
    for cut in pieces[1:]:
        gain = gain * one(*cut)
    return gain


def scatter_about(rng, dims, width, most, split=(), kind=jnp.bfloat16):
    result = width * jax.random.normal(rng, dims, jnp.float32)
    if split:
        result = result * levels(rng, dims, split, -0.22, 0.18)
    return jnp.clip(result, -most, most).astype(kind)


def bell_draw_with(rng, extent, scale, reach, split, heavy, held_as=jnp.bfloat16):
    entries = scale * jax.random.normal(rng, extent, jnp.float32)
    if split:
        entries = entries * levels(rng, extent, split, -0.22, 0.18)
    return jnp.clip(strengthened(entries, jax.random.fold_in(rng, 3), *heavy), -reach, reach).astype(held_as)


def setup_inputs(seed: int = 0) -> dict:
    splits = jax.random.split(jax.random.key(seed), 16)
    inputs = scatter_about(splits[0], (SEQS, LENGTH, D), 1.0, 6.0, ((0, 2), (1, 4)))
    cotangent = bell_draw_with(splits[1], (SEQS, LENGTH, D), 1.0, 6.0, ((0, 2), (1, 4)), (0, 2, 2, 2.0))
    piece_starts = draw_piece_starts(jax.random.fold_in(splits[15], 71), 0)
    positions = draw_positions(jax.random.fold_in(splits[15], 71), 0)
    w_qkv = scatter_about(splits[4], (D, HEADS, 3 * HEAD), D ** -0.5, 0.125, ((0, 8), (1, 4)), jnp.float32)
    b_qkv = scatter_about(splits[5], (HEADS, 3 * HEAD), 0.2, 1.2, ((0, 4),), jnp.float32)
    w_dense = scatter_about(splits[6], (D, HEADS, HEAD), (D // 16) ** -0.5, 0.5, ((0, 8), (1, 4)), jnp.float32)
    w_fc1 = scatter_about(splits[7], (D, FF), D ** -0.5, 0.125, ((0, 8), (1, 4)), jnp.float32)
    b_fc1 = scatter_about(splits[8], (FF,), 0.5, 3.0, ((0, 4),), jnp.float32)
    w_fc2 = scatter_about(splits[9], (D, FF), FF ** -0.5, 0.0625, ((0, 8), (1, 4)), jnp.float32)
    out_bias = scatter_about(splits[10], (D,), 0.5, 3.0, (), jnp.float32)
    ln1_gain = jnp.clip(1.0 + 0.18 * jax.random.normal(splits[11], (D,), jnp.float32), 0.1, 1.9)
    ln1_bias = scatter_about(splits[12], (D,), 0.3, 2.0, (), jnp.float32)
    ln2_gain = jnp.clip(1.0 + 0.18 * jax.random.normal(splits[13], (D,), jnp.float32), 0.1, 1.9)
    ln2_bias = scatter_about(splits[14], (D,), 0.3, 2.0, (), jnp.float32)
    return {"inputs": inputs, "cotangent": cotangent, "piece_starts": piece_starts, "positions": positions, "w_qkv": w_qkv, "b_qkv": b_qkv, "w_dense": w_dense, "w_fc1": w_fc1, "b_fc1": b_fc1, "w_fc2": w_fc2, "out_bias": out_bias, "ln1_gain": ln1_gain, "ln1_bias": ln1_bias, "ln2_gain": ln2_gain, "ln2_bias": ln2_bias}


EPSILON = 1e-05
ROPE_BASE = 10000.0

@jax.custom_vjp
def low(v):
    return lax.optimization_barrier(v.astype(jnp.bfloat16)).astype(jnp.float32)

@jax.custom_vjp
def low_back(v):
    return v

def low_keep(v):
    return (low(v), None)

def low_pass(kept, grad):
    return (grad,)

def back_keep(v):
    return (v, None)

def back_low(kept, grad):
    return (low(grad),)
low.defvjp(low_keep, low_pass)
low_back.defvjp(back_keep, back_low)

def matmul(left_side, right_side):
    return jnp.dot(left_side, right_side, precision=lax.Precision.HIGHEST, preferred_element_type=jnp.float32)

def layer_norm(values, norm_gain, norm_shift):
    centred = values - lax.optimization_barrier(jnp.mean(values, axis=-1, keepdims=True))
    spread = lax.optimization_barrier(jnp.mean(centred * centred, axis=-1, keepdims=True))
    return centred * lax.rsqrt(spread + EPSILON) * norm_gain + norm_shift

def rotary_tables(places):
    half_rot = ROT // 2
    frequency = ROPE_BASE ** (-(jnp.arange(half_rot, dtype=jnp.float32) * 2.0) / ROT)
    angles = places.astype(jnp.float32)[..., None] * frequency
    angles = jnp.concatenate([angles, angles], axis=-1)
    return (jnp.cos(angles)[..., None, :], jnp.sin(angles)[..., None, :])

def rotate(head_values, cosine, sine_part):
    half_rot = ROT // 2
    rotated_part = head_values[..., :ROT]
    turned = jnp.concatenate([-rotated_part[..., half_rot:], rotated_part[..., :half_rot]], axis=-1)
    return jnp.concatenate([rotated_part * cosine + turned * sine_part, head_values[..., ROT:]], axis=-1)

def piece_ids(token_index, starts):
    inside = (token_index[:, None] >= starts[None, :]) & (token_index[:, None] < starts[None, :] + PIECE)
    labels = jnp.arange(1, PIECES + 1, dtype=jnp.int32)
    return lax.optimization_barrier(jnp.sum(jnp.where(inside, labels[None, :], 0), axis=1)).astype(jnp.int32)

def sequence_forward(parameters, values, starts, places):
    w_qkv, b_qkv, w_dense, w_fc1, b_fc1, w_fc2, out_bias, ln1_gain, ln1_bias, ln2_gain, ln2_bias = parameters
    normed_one = low(layer_norm(values, ln1_gain, ln1_bias))
    normed_two = low(layer_norm(values, ln2_gain, ln2_bias))
    joined = matmul(normed_one, low(w_qkv).reshape(D, HEADS * 3 * HEAD)).reshape(LENGTH, HEADS, 3 * HEAD)
    joined = low_back(joined + b_qkv)
    cosine, sine_part = rotary_tables(places)
    queries = low(rotate(joined[..., :HEAD], cosine, sine_part))
    key_rows = low(rotate(joined[..., HEAD:2 * HEAD], cosine, sine_part))
    value_rows = low(joined[..., 2 * HEAD:])
    token_index = jnp.arange(LENGTH, dtype=jnp.int32)
    piece_labels = piece_ids(token_index, starts)
    block_rows = min(512, LENGTH)
    score_scale = HEAD ** (-0.5)

    def attend(block_item):
        query_block, query_index, query_piece = block_item
        scores = jnp.einsum('qhd,khd->hqk', query_block, key_rows, precision=lax.Precision.HIGHEST) * score_scale
        scores = low_back(scores)
        allowed = (token_index[None, :] <= query_index[:, None]) | (piece_labels[None, :] == query_piece[:, None]) & (query_piece[:, None] > 0)
        scores = jnp.where(allowed[None], scores, -1e+30)
        weights = low(jax.nn.softmax(scores, axis=-1))
        return jnp.einsum('hqk,khd->qhd', weights, value_rows, precision=lax.Precision.HIGHEST)
    attended = lax.map(jax.checkpoint(attend), (queries.reshape(LENGTH // block_rows, block_rows, HEADS, HEAD), token_index.reshape(-1, block_rows), piece_labels.reshape(-1, block_rows)))
    context = low(low_back(attended.reshape(LENGTH, HEADS * HEAD)))
    attn_out = matmul(context, low(w_dense).reshape(D, HEADS * HEAD).T)
    pre_gelu = low_back(matmul(normed_two, low(w_fc1)) + b_fc1)
    hidden = low(jax.nn.gelu(pre_gelu, approximate=False))
    mlp_out = matmul(hidden, low(w_fc2).T)
    return values + attn_out + mlp_out + out_bias

def add_pair(first_term, second_term):
    return first_term + second_term

def reference(inputs, cotangent, piece_starts, positions, w_qkv, b_qkv, w_dense, w_fc1, b_fc1, w_fc2, out_bias, ln1_gain, ln1_bias, ln2_gain, ln2_bias):
    parameters = tuple((item.astype(jnp.float32) for item in (w_qkv, b_qkv, w_dense, w_fc1, b_fc1, w_fc2, out_bias, ln1_gain, ln1_bias, ln2_gain, ln2_bias)))

    def per_sequence(totals, seq_item):
        seq_values, seq_grad, starts, places = seq_item

        def forward(params_in, values_in):
            return sequence_forward(params_in, values_in, starts, places)
        seq_out, pullback = jax.vjp(forward, parameters, seq_values.astype(jnp.float32))
        grad_params, grad_values = pullback(seq_grad.astype(jnp.float32))
        totals = jax.tree.map(add_pair, totals, grad_params)
        return (totals, (seq_out.astype(jnp.bfloat16), grad_values))
    zero_totals = jax.tree.map(jnp.zeros_like, parameters)
    totals, (outputs, input_grads) = lax.scan(per_sequence, zero_totals, (inputs, cotangent, piece_starts, positions))
    return (outputs, input_grads, totals[0], totals[1], totals[2], totals[3], totals[4], totals[5], totals[6], totals[7], totals[8], totals[9], totals[10])
```

```python
import jax
import jax.numpy as jnp
from jax import lax
from jax.sharding import PartitionSpec as P

HEAD = 256
ROT = 64
PIECE = 256
PIECES = 3

EPSILON = 1e-05
ROPE_BASE = 10000.0
LOW = jnp.bfloat16
WIDE = jnp.float32


def rotary_tables(places):
    half_rot = ROT // 2
    frequency = ROPE_BASE ** (-(jnp.arange(half_rot, dtype=WIDE) * 2.0) / ROT)
    angles = places.astype(WIDE)[..., None] * frequency
    angles = jnp.concatenate([angles, angles], axis=-1)
    return (jnp.cos(angles), jnp.sin(angles))


def rotate(head_values, cosine, sine_part):
    half_rot = ROT // 2
    rotated_part = head_values[..., :ROT]
    turned = jnp.concatenate([-rotated_part[..., half_rot:], rotated_part[..., :half_rot]], axis=-1)
    return jnp.concatenate(
        [rotated_part * cosine + turned * sine_part, head_values[..., ROT:]], axis=-1
    )


def piece_of(token_index, starts):
    inside = (token_index[:, None] >= starts[None, :]) & (token_index[:, None] < starts[None, :] + PIECE)
    labels = jnp.arange(1, PIECES + 1, dtype=jnp.int32)
    return jnp.sum(jnp.where(inside, labels, 0), axis=1)


def exact_gelu(pre_act):
    return jax.nn.gelu(pre_act, approximate=False)


def mm(a, b):
    return jnp.dot(a, b, preferred_element_type=WIDE)


def mm_nt(a, b):
    return lax.dot_general(a, b, (((1,), (1,)), ((), ())), preferred_element_type=WIDE)


def mm_tn(a, b):
    return lax.dot_general(a, b, (((0,), (0,)), ((), ())), preferred_element_type=WIDE)


SWAP_X = [(0, 2), (2, 0), (1, 3), (3, 1)]
SWAP_C = [(0, 1), (1, 0), (2, 3), (3, 2)]


def swap_x(v):
    return lax.ppermute(v, "ctx", SWAP_X)


def swap_c(v):
    return lax.ppermute(v, "ctx", SWAP_C)


def local(
    inputs,
    cotangent,
    piece_starts,
    positions,
    w_qkv,
    b_qkv,
    w_dense,
    w_fc1,
    b_fc1,
    w_fc2,
    out_bias,
    ln1_gain,
    ln1_bias,
    ln2_gain,
    ln2_bias,
):
    shards = lax.axis_size("shard")
    tensors = lax.axis_size("tensor")
    shard = lax.axis_index("shard")
    ctx = lax.axis_index("ctx")
    tensor = lax.axis_index("tensor")
    here_x = ctx // 2
    here_c = ctx % 2
    n = inputs.shape[1]
    width = inputs.shape[2]
    rows = w_fc1.shape[0]
    hid = w_fc1.shape[1] // 2
    scale = HEAD ** (-0.5)

    rel = [(dc, ds, dx) for dc in range(2) for ds in range(shards) for dx in range(2)]
    rel_abs = [
        (lax.rem(shard + ds, shards) * 2 + (here_x ^ dx)) * 2 + (here_c ^ dc) for dc, ds, dx in rel
    ]
    abs_rel = [
        ((here_c ^ cb) * shards + lax.rem(sb - shard + shards, shards)) * 2 + (here_x ^ xb)
        for sb in range(shards)
        for xb in range(2)
        for cb in range(2)
    ]

    def blocks_at(v, order):
        return jnp.concatenate(
            [lax.dynamic_slice_in_dim(v, b * rows, rows, axis=v.ndim - 1) for b in order], axis=-1
        )

    def to_rel(v):
        return blocks_at(v, rel_abs)

    def from_rel(v):
        return blocks_at(v, abs_rel)

    def flip_x(v):
        return jnp.concatenate(
            [v[..., (j ^ 1) * rows : ((j ^ 1) + 1) * rows] for j in range(2 * 2 * shards)], axis=-1
        )

    def from_shard(v, ds):
        return lax.ppermute(v, "shard", [((j + ds) % shards, j) for j in range(shards)])

    def to_shard(v, ds):
        return lax.ppermute(v, "shard", [(j, (j + ds) % shards) for j in range(shards)])

    def gather_rows(keep, send):
        other = swap_x(send)
        near = [keep, other]
        for ds in range(1, shards):
            near += [from_shard(keep, ds), from_shard(other, ds)]
        far = [swap_c(v) for v in near]
        return jnp.concatenate(near + far, axis=0)

    def halves(w):
        keep = lax.dynamic_slice_in_dim(w, here_x * hid, hid, axis=1).astype(LOW)
        send = lax.dynamic_slice_in_dim(w, (1 - here_x) * hid, hid, axis=1).astype(LOW)
        return keep, send

    def head_of(w, which):
        return lax.dynamic_index_in_dim(w, which, axis=1, keepdims=False)

    x_own = to_rel(inputs[0])
    cot_own = to_rel(cotangent[0])
    qkv_all = gather_rows(head_of(w_qkv, here_x).astype(LOW), head_of(w_qkv, 1 - here_x).astype(LOW))
    x_oth = flip_x(swap_x(x_own))
    fc1_all = gather_rows(*halves(w_fc1))
    cot_oth = flip_x(swap_x(cot_own))
    dense_all = gather_rows(
        head_of(w_dense, here_x).astype(LOW), head_of(w_dense, 1 - here_x).astype(LOW)
    )
    fc2_all = gather_rows(*halves(w_fc2))
    places = jnp.concatenate([positions[0], swap_x(positions[0])])

    gain1, shift1, gain2, shift2 = (to_rel(v) for v in (ln1_gain, ln1_bias, ln2_gain, ln2_bias))
    residual = jnp.concatenate([x_own, x_oth], axis=0).astype(WIDE)
    centred = residual - jnp.mean(residual, axis=-1, keepdims=True)
    inv_std = lax.rsqrt(jnp.mean(centred * centred, axis=-1, keepdims=True) + EPSILON)
    normal = centred * inv_std
    normed_one = (normal * gain1 + shift1).astype(LOW)
    normed_two = (normal * gain2 + shift2).astype(LOW)
    cot = jnp.concatenate([cot_own, cot_oth], axis=0)

    bias_fc1 = lax.dynamic_slice_in_dim(b_fc1, here_x * hid, hid)
    pre_gelu = mm(normed_two, fc1_all) + bias_fc1
    hidden = exact_gelu(pre_gelu).astype(LOW)

    joined = mm(normed_one, qkv_all) + lax.dynamic_index_in_dim(b_qkv, here_x, keepdims=False)
    cosine, sine_part = rotary_tables(places)
    queries = rotate(joined[:, :HEAD], cosine, sine_part).astype(LOW)
    key_rows = rotate(joined[:, HEAD : 2 * HEAD], cosine, sine_part).astype(LOW)
    value_rows = joined[:, 2 * HEAD :].astype(LOW)
    kv = jnp.concatenate([key_rows, value_rows], axis=1)
    kv_all = jnp.concatenate([kv, swap_c(kv)], axis=0)
    all_keys, all_values = kv_all[:, :HEAD], kv_all[:, HEAD:]
    token = jnp.arange(n, dtype=jnp.int32)
    q_index = jnp.concatenate([ctx * n + token, (ctx ^ 2) * n + token])
    k_index = jnp.concatenate([q_index, (ctx ^ 1) * n + token, (ctx ^ 3) * n + token])
    starts = piece_starts[0]
    q_piece = piece_of(q_index, starts)
    k_piece = piece_of(k_index, starts)
    allowed = (k_index[None, :] <= q_index[:, None]) | (
        (k_piece[None, :] == q_piece[:, None]) & (q_piece[:, None] > 0)
    )
    scores = jnp.where(allowed, mm_nt(queries, all_keys) * scale, -1e30)
    exponent = jnp.exp(scores - jnp.max(scores, axis=-1, keepdims=True))
    probs = exponent / jnp.sum(exponent, axis=-1, keepdims=True)
    probs_low = probs.astype(LOW)
    context = mm(probs_low, all_values).astype(LOW)

    block_out = (mm_nt(context, dense_all) + mm_nt(hidden, fc2_all)).astype(LOW)
    out_sum = block_out[:n].astype(WIDE) + swap_x(flip_x(block_out[n:])).astype(WIDE)

    part = n // tensors

    def sum_tensor(v):
        v = v.astype(LOW)

        def chunk(k):
            return lax.dynamic_slice_in_dim(v, lax.rem(tensor + k, tensors) * part, part, axis=0)

        total = chunk(0).astype(WIDE)
        for k in range(1, tensors):
            got = lax.ppermute(
                chunk(k), "tensor", [(j, (j + k) % tensors) for j in range(tensors)]
            )
            total = total + got.astype(WIDE)
        return total

    def gather_tensor(v):
        full = jnp.zeros((n, v.shape[1]), v.dtype)
        full = lax.dynamic_update_slice_in_dim(full, v, tensor * part, axis=0)
        for k in range(1, tensors):
            got = lax.ppermute(v, "tensor", [(j, (j + k) % tensors) for j in range(tensors)])
            at = lax.rem(tensor - k + tensors, tensors) * part
            full = lax.dynamic_update_slice_in_dim(full, got, at, axis=0)
        return full

    def my_rows(v):
        return lax.dynamic_slice_in_dim(v, tensor * part, part, axis=0)

    out_rows = my_rows(x_own).astype(WIDE) + sum_tensor(out_sum) + to_rel(out_bias)
    output = from_rel(gather_tensor(out_rows.astype(LOW)))

    def give_rows(grad):
        half = width // 2
        total = grad[:half] + swap_c(grad[half:].astype(LOW)).astype(WIDE)
        mine = total[: 2 * rows]
        for ds in range(1, shards):
            sent = total[2 * rows * ds : 2 * rows * (ds + 1)].astype(LOW)
            mine = mine + to_shard(sent, ds).astype(WIDE)
        return mine[:rows], swap_x(mine[rows:].astype(LOW)).astype(WIDE)

    def join_cols(pair):
        return jnp.where(
            here_x == 0, jnp.concatenate(pair, axis=1), jnp.concatenate(pair[::-1], axis=1)
        )

    def join_heads(pair):
        head = lax.broadcasted_iota(jnp.int32, (1, 2, 1), 1)
        return jnp.where(head == here_x, pair[0][:, None], pair[1][:, None])

    grad_w_fc2 = join_cols(give_rows(mm_tn(cot, hidden)))
    grad_w_dense = join_heads(give_rows(mm_tn(cot, context)))

    grad_hidden = mm(cot, fc2_all)
    grad_inner = jax.vjp(exact_gelu, pre_gelu)[1](grad_hidden)[0].astype(LOW)
    grad_w_fc1 = join_cols(give_rows(mm_tn(normed_two, grad_inner)))

    grad_mixed = mm(cot, dense_all).astype(LOW)
    grad_probs = mm_nt(grad_mixed, all_values)
    centre = jnp.sum(probs * grad_probs, axis=-1, keepdims=True)
    grad_scores = (probs * (grad_probs - centre)).astype(LOW)
    grad_queries = mm(grad_scores, all_keys) * scale
    key_terms = mm_tn(grad_scores, queries) * scale
    value_terms = mm_tn(probs_low, grad_mixed)
    kv_terms = jnp.concatenate([key_terms, value_terms], axis=1)
    kv_grad = kv_terms[: 2 * n] + swap_c(kv_terms[2 * n :])
    grad_joined = jnp.concatenate(
        [
            rotate(grad_queries, cosine, -sine_part),
            rotate(kv_grad[:, :HEAD], cosine, -sine_part),
            kv_grad[:, HEAD:],
        ],
        axis=-1,
    ).astype(LOW)
    grad_w_qkv = join_heads(give_rows(mm_tn(normed_one, grad_joined)))

    grad_one = mm_nt(grad_joined, qkv_all)
    grad_two = mm_nt(grad_inner, fc1_all)
    mixed = (grad_one * gain1 + grad_two * gain2).astype(LOW)
    mixed_sum = mixed[:n].astype(WIDE) + swap_x(flip_x(mixed[n:])).astype(WIDE)
    h = sum_tensor(mixed_sum)
    n_rows = my_rows(normal[:n])
    back = (
        h - jnp.mean(h, axis=-1, keepdims=True) - n_rows * jnp.mean(h * n_rows, axis=-1, keepdims=True)
    ) * my_rows(inv_std[:n])
    grad_inputs = cotangent[0].astype(WIDE) + from_rel(gather_tensor(back.astype(LOW))).astype(WIDE)

    def at_half(v, size):
        return lax.dynamic_update_slice_in_dim(jnp.zeros((2,) + v.shape, WIDE), v[None], here_x, axis=0)

    wide_sums = lax.psum(
        tuple(
            from_rel(v)
            for v in (
                jnp.where(tensor == 0, jnp.sum(cot_own.astype(WIDE), axis=0), 0.0),
                jnp.sum(grad_one * normal, axis=0),
                jnp.sum(grad_one, axis=0),
                jnp.sum(grad_two * normal, axis=0),
                jnp.sum(grad_two, axis=0),
            )
        ),
        ("shard", "ctx", "tensor"),
    )
    grad_b_qkv, grad_b_fc1 = lax.psum(
        (
            at_half(jnp.sum(grad_joined.astype(WIDE), axis=0), 3 * HEAD),
            at_half(jnp.sum(grad_inner.astype(WIDE), axis=0), hid),
        ),
        ("shard", "ctx"),
    )
    return (
        output[None],
        grad_inputs[None],
        grad_w_qkv,
        grad_b_qkv,
        grad_w_dense,
        grad_w_fc1,
        grad_b_fc1.reshape(2 * hid),
        grad_w_fc2,
        *wide_sums,
    )


def solution(mesh):
    rows = P(("shard", "ctx"), "tensor")
    in_specs = (
        P("shard", "ctx", None),
        P("shard", "ctx", None),
        P("shard", None),
        P("shard", "ctx"),
        P(("shard", "ctx"), "tensor", None),
        P("tensor", None),
        P(("shard", "ctx"), "tensor", None),
        rows,
        P("tensor"),
        rows,
        P(),
        P(),
        P(),
        P(),
        P(),
    )
    out_specs = (
        P("shard", "ctx", None),
        P("shard", "ctx", None),
        P(("shard", "ctx"), "tensor", None),
        P("tensor", None),
        P(("shard", "ctx"), "tensor", None),
        rows,
        P("tensor"),
        rows,
        P(),
        P(),
        P(),
        P(),
        P(),
    )
    return jax.shard_map(local, mesh=mesh, in_specs=in_specs, out_specs=out_specs, check_vma=False)
```
